32 devices in a mesh: dp: 4 (over x, core), expert: 8 (over z, y).
Axes of the slice: x: 2, y: 2, z: 4, core: 2. Of those that a mesh axis runs over, the one named last changes fastest.
Arguments:
- grad_partials: bfloat16 [4, 7168, 8192], P('dp', None, 'expert'), may hold values from -6 to 6
- master_weights: float32 [7168, 8192], P('dp', 'expert'), may hold values from -0.3125 to 0.3125
- first_moment: float32 [7168, 8192], P('dp', 'expert'), may hold values from -2 to 2
- second_moment: float32 [7168, 8192], P('dp', 'expert'), may hold values from 0.02 to 0.5
- resident_weights: bfloat16 [7168, 16384], P('dp', 'expert'), may hold values from -0.6 to 0.6
- token_tiles: bfloat16 [8192, 7168], P('expert', 'dp'), may hold values from -6 to 6
- owner_expert: int32 [8], replicated, may hold values from 0 to 3, as said below
- live_rows: int32 [8], P('expert'), may hold values from 256 to 1024, as said below
Outputs:
- updated_master: float32 [7168, 8192], P('dp', 'expert')
- projected: bfloat16 [8192, 2048], P('expert', 'dp')
The draws below stay inside these ranges and needn't reach their ends.
Inputs may be any that keep to these rules, and one draw needn't show every extreme that they name: `owner_expert`: each owner hosts one of the 4 experts; every expert is hosted by at least one owner, some by several. The first live_rows[o] of owner o's rows are live; some owner has all 1024 rows live.
All inputs are finite; a program needn't handle non-finite values.
Results may differ from the reference program's by a relative error of at most 0.035.
Values may be sent and summed in bfloat16 or wider, within the bound.
No kernel may reach another device: no remote copies, remote signals or barrier semaphores. Data moves between devices by JAX's collectives and lax.ppermute only.
A program may use at most 192 MiB of HBM per device.

```python
import math
import jax
import jax.numpy as jnp
from jax import lax

D = 7168
F = 2048
EXPERTS = 4
QB = 128
ROWS = 1024
OWNERS = 8
OWNER_COLS = 16384
OWNER_ROWS = 8192
N_DP = 4
N_EXPERT = 8


def draw_resident_weights(key, part):
    subkeys = jax.random.split(jax.random.fold_in(key, 11), 3)
    values = jnp.clip(jax.random.normal(subkeys[0], (D, OWNER_COLS), jnp.float32), -6.0, 6.0)
    low_end = 0.316
    high_end = 3.16
    row_scale = jnp.exp(jax.random.uniform(subkeys[1], (D, 1), jnp.float32, math.log(low_end), math.log(high_end)))
    col_scale = jnp.exp(jax.random.uniform(subkeys[2], (1, OWNER_COLS), jnp.float32, math.log(low_end), math.log(high_end)))
    return (0.01 * values * row_scale * col_scale).astype(jnp.bfloat16)


def draw_owner_expert(key, part):
    subkeys = jax.random.split(jax.random.fold_in(key, 23), 4)
    owners_list = jnp.arange(OWNERS, dtype=jnp.int32)
    first_draw = jax.random.randint(subkeys[0], (OWNERS,), 0, EXPERTS, dtype=jnp.int32)
    second_draw = jax.random.randint(subkeys[1], (OWNERS,), 0, EXPERTS, dtype=jnp.int32)
    skewed = jnp.minimum(first_draw, second_draw)
    labels = jnp.where(owners_list < EXPERTS, owners_list, skewed)
    relabel = jax.random.permutation(subkeys[2], EXPERTS).astype(jnp.int32)
    labels = relabel[labels]
    placement_order = jax.random.permutation(subkeys[3], OWNERS).astype(jnp.int32)
    return jnp.zeros((OWNERS,), jnp.int32).at[placement_order].set(labels)


def draw_live_rows(key, part):
    subkeys = jax.random.split(jax.random.fold_in(key, 37), 2)
    counts = jax.random.randint(subkeys[0], (OWNERS,), ROWS // 4, ROWS + 1, dtype=jnp.int32)
    full_owner = jax.random.randint(subkeys[1], (), 0, OWNERS, dtype=jnp.int32)
    return counts.at[full_owner].set(ROWS)


def raised(array, rng, source, target, parts, factor):
    def block_of(dim):
        return (jnp.arange(array.shape[dim]) // (array.shape[dim] // parts)).reshape((-1,) + (1,) * (array.ndim - 1 - dim))

    one_side = jax.random.permutation(rng, parts)[block_of(target)]
    second = (block_of(target) + parts // 2) % parts
    return jnp.where((block_of(source) == one_side) | (block_of(source) == second), factor * array, array)


def shard_levels(stream_key, shape, shards, smallest, high):
    gain = 1.0
    for axis_at, parts in shards:
        heights = jax.random.uniform(jax.random.fold_in(jax.random.fold_in(stream_key, 6), axis_at), (parts,), jnp.float32, smallest / len(shards), high / len(shards))
        gain = gain * jnp.repeat(jnp.exp(heights), shape[axis_at] // parts).reshape((-1,) + (1,) * (len(shape) - 1 - axis_at))
    return gain


def gaussian(key, dims, width, limit, shards=(), held_as=jnp.bfloat16):
    factor_of = shard_levels(key, dims, shards, -0.22, 0.18) if shards else 1.0
    entries = jax.random.normal(key, dims, jnp.float32) * width * factor_of
    return jnp.minimum(jnp.maximum(entries, -limit), limit).astype(held_as)


def bell_draw_with(rng, extent, width, most, pieces, heavy, kind=jnp.bfloat16):
    entries = width * jax.random.normal(rng, extent, jnp.float32)
    if pieces:
        entries = entries * shard_levels(rng, extent, pieces, -0.22, 0.18)
    return jnp.clip(raised(entries, jax.random.fold_in(rng, 3), *heavy), -most, most).astype(kind)


def setup_inputs(seed: int = 0) -> dict:
    streams_of = jax.random.split(jax.random.key(seed), 9)
    grad_partials = bell_draw_with(streams_of[0], (N_DP, D, EXPERTS * F), 0.5, 6.0, ((0, 4), (2, 8)), (0, 1, 4, 2.0))
    master_weights = gaussian(streams_of[1], (D, EXPERTS * F), 0.02, 0.3125, ((0, 4), (1, 8)), jnp.float32)
    first_moment = gaussian(streams_of[2], (D, EXPERTS * F), 0.15, 2.0, ((0, 4), (1, 8)), jnp.float32)
    second_moment = jnp.clip(jnp.exp(math.log(0.5) - 3.218876 * jax.random.uniform(streams_of[3], (D, EXPERTS * F), jnp.float32) ** shard_levels(streams_of[3], (D, EXPERTS * F), ((0, 4), (1, 8)), -0.2, 0.2)), 0.02, 0.5)
    resident_weights = draw_resident_weights(jax.random.fold_in(streams_of[8], 71), 0)
    token_tiles = gaussian(streams_of[5], (OWNER_ROWS, D), 1.0, 6.0, ((0, 8), (1, 4)))
    owner_expert = draw_owner_expert(jax.random.fold_in(streams_of[8], 71), 0)
    live_rows = draw_live_rows(jax.random.fold_in(streams_of[8], 71), 0)
    return dict(grad_partials=grad_partials, master_weights=master_weights, first_moment=first_moment, second_moment=second_moment, resident_weights=resident_weights, token_tiles=token_tiles, owner_expert=owner_expert, live_rows=live_rows)


beta_first = 0.9
beta_second = 0.95
learn_rate = 0.02
decay_rate = 0.1
adam_epsilon = 1e-08
scale_epsilon = 1e-06
quant_range = 448.0
grid_step = 8.0
bias_first = 1.0 - 0.9 ** 20
bias_second = 1.0 - 0.95 ** 20

def adamw(gradient, master_weights, first_moment, second_moment):
    moment_one = beta_first * first_moment + (1.0 - beta_first) * gradient
    moment_two = beta_second * second_moment + (1.0 - beta_second) * gradient * gradient
    update = moment_one / bias_first / (jnp.sqrt(moment_two / bias_second) + adam_epsilon)
    return master_weights - learn_rate * (update + decay_rate * master_weights)

def quantize(weight):
    rows_total, cols_total = weight.shape
    blocks = weight.reshape(rows_total // QB, QB, cols_total // QB, QB)
    largest = lax.optimization_barrier(jnp.max(jnp.abs(blocks), axis=(1, 3)))
    scales = (largest + scale_epsilon) / quant_range
    ratio = blocks / scales[:, None, :, None]
    level = grid_step * jnp.floor(ratio / grid_step + 0.5)
    return (level, scales)

def reference(grad_partials, master_weights, first_moment, second_moment, resident_weights, token_tiles, owner_expert, live_rows):
    gradient = jnp.zeros(master_weights.shape, jnp.float32)
    for replica in range(N_DP):
        gradient = gradient + grad_partials[replica].astype(jnp.float32)
    updated_master = adamw(gradient, master_weights, first_moment, second_moment)
    delta = (updated_master - master_weights).astype(jnp.bfloat16)
    tiles_owned = token_tiles.reshape(N_EXPERT, ROWS, D)
    slab_rows = D // N_DP

    def serve(inputs):
        owner_index, expert_index, tile_block, live_count = inputs
        resident = lax.dynamic_slice_in_dim(resident_weights, (owner_index * F).astype(jnp.int32), F, 1).astype(jnp.float32)
        change = lax.dynamic_slice_in_dim(delta, (expert_index * F).astype(jnp.int32), F, 1).astype(jnp.float32)
        level, scales = quantize(resident + change)
        dequant = (level * scales[:, None, :, None]).reshape(N_DP, slab_rows, F)
        tile_slabs = tile_block.astype(jnp.float32).reshape(ROWS, N_DP, slab_rows)
        partials = jnp.einsum('rgd,gdf->grf', tile_slabs, dequant, precision=lax.Precision.HIGHEST)
        rounded = lax.optimization_barrier(partials.astype(jnp.bfloat16))
        product = lax.optimization_barrier(jnp.sum(rounded.astype(jnp.float32), axis=0))
        row_index = jnp.arange(ROWS, dtype=jnp.int32)[:, None]
        return jnp.where(row_index < live_count, product, jnp.float32(0.0)).astype(jnp.bfloat16)
    owners_list = jnp.arange(N_EXPERT, dtype=jnp.int32)
    projected = lax.map(serve, (owners_list, owner_expert.astype(jnp.int32), tiles_owned, live_rows.astype(jnp.int32)))
    return (updated_master, projected.reshape(N_EXPERT * ROWS, F))
```

```python
import functools

import jax
import jax.numpy as jnp
from jax import lax
from jax.experimental import pallas as pl
from jax.experimental.pallas import tpu as pltpu
from jax.sharding import PartitionSpec as P

EXPERTS = 4
QB = 128

beta_first = 0.9
beta_second = 0.95
learn_rate = 0.02
decay_rate = 0.1
adam_epsilon = 1e-08
scale_epsilon = 1e-06
quant_range = 448.0
grid_step = 8.0
bias_first = 1.0 - 0.9**20
bias_second = 1.0 - 0.95**20

VMEM_BYTES = 24 << 20
ROW_PARTS = 2


def adamw(gradient, master_weights, first_moment, second_moment):
    moment_one = beta_first * first_moment + (1.0 - beta_first) * gradient
    moment_two = beta_second * second_moment + (1.0 - beta_second) * gradient * gradient
    update = moment_one / bias_first / (jnp.sqrt(moment_two / bias_second) + adam_epsilon)
    return master_weights - learn_rate * (update + decay_rate * master_weights)


def params(**kw):
    return pltpu.CompilerParams(vmem_limit_bytes=VMEM_BYTES, **kw)


def total(refs):
    value = refs[0].astype(jnp.float32)
    for ref in refs[1:]:
        value = value + ref.astype(jnp.float32)
    return value


def slab_sum(grad, slabs, received, rows, part_rows, part, cols, width):
    n_out = slabs.shape[0]
    n_cols = len(cols)
    block = part_rows
    step = rows // block
    n_rows = part_rows // block

    def kernel(tab, *refs):
        grads, recs, out = refs[:n_cols], refs[n_cols:-1], refs[-1]
        for k in range(n_cols):
            span = slice(k * width, (k + 1) * width)
            values = [grads[k][...]] + [rec[0, :, span] for rec in recs]
            out[0, :, span] = total(values).astype(out.dtype)

    def grad_map(k):
        at = cols[k] // width
        return lambda i, r, tab: (tab[i] * step + part * n_rows + r, at)

    def rec_map(stride, offset, first):
        return lambda i, r, tab: (first + i * stride, offset * n_rows + r, 0)

    in_specs = [pl.BlockSpec((block, width), grad_map(k)) for k in range(n_cols)]
    in_specs += [
        pl.BlockSpec((1, block, n_cols * width), rec_map(stride, offset, first))
        for (_, offset, first, stride) in received
    ]
    moved = n_out * part_rows * n_cols * width * 2
    return pl.pallas_call(
        kernel,
        grid_spec=pltpu.PrefetchScalarGridSpec(
            num_scalar_prefetch=1,
            grid=(n_out, n_rows),
            in_specs=in_specs,
            out_specs=pl.BlockSpec((1, block, n_cols * width), lambda i, r, tab: (i, r, 0)),
        ),
        out_shape=jax.ShapeDtypeStruct((n_out, part_rows, n_cols * width), jnp.bfloat16),
        compiler_params=params(),
        cost_estimate=pl.CostEstimate(
            flops=moved, bytes_accessed=moved * (2 + len(received)), transcendentals=0
        ),
        name="slab_sum",
    )(slabs, *([grad] * n_cols), *[item[0] for item in received])


def adam_part(grad, slab, received, state, out, rows, part_rows, part, cols, width):
    n_cols = len(cols)
    block = part_rows // 2 if part_rows % (2 * 16) == 0 else part_rows
    step = rows // block
    n_rows = part_rows // block
    base = cols[0] // width
    stride = (cols[1] - cols[0]) // width if n_cols > 1 else 0
    n_rec = len(received)

    def kernel(tab, grad_ref, *refs):
        recs = refs[:n_rec]
        master, first, second = refs[n_rec : n_rec + 3]
        new_ref, delta_ref = refs[-2:]
        gradient = total([grad_ref[...]] + [rec[0] for rec in recs])
        old = master[...]
        new = adamw(gradient, old, first[...], second[...])
        new_ref[...] = new
        delta_ref[...] = (new - old).astype(delta_ref.dtype)

    def state_map(r, k, tab):
        return (part * n_rows + r, base + k * stride)

    state_spec = pl.BlockSpec((block, width), state_map)
    in_specs = [
        pl.BlockSpec(
            (block, width), lambda r, k, tab: (tab[0] * step + part * n_rows + r, base + k * stride)
        )
    ]

    def rec_map(offset):
        return lambda r, k, tab: (0, offset * n_rows + r, k)

    in_specs += [pl.BlockSpec((1, block, width), rec_map(offset)) for (_, offset) in received]
    in_specs += [state_spec] * 3
    operands = [slab, grad, *[item[0] for item in received], *state]
    aliases = {}
    if out is not None:
        in_specs.append(pl.BlockSpec(memory_space=pl.ANY))
        aliases = {len(operands): 0}
        operands.append(out)
    count = part_rows * n_cols * width
    return pl.pallas_call(
        kernel,
        grid_spec=pltpu.PrefetchScalarGridSpec(
            num_scalar_prefetch=1,
            grid=(n_rows, n_cols),
            in_specs=in_specs,
            out_specs=(
                state_spec,
                pl.BlockSpec((block, width), lambda r, k, tab: (r, k)),
            ),
        ),
        out_shape=(
            jax.ShapeDtypeStruct(state[0].shape, jnp.float32),
            jax.ShapeDtypeStruct((part_rows, n_cols * width), jnp.bfloat16),
        ),
        input_output_aliases=aliases,
        compiler_params=params(),
        cost_estimate=pl.CostEstimate(
            flops=30 * count, bytes_accessed=(20 + 2 * n_rec) * count, transcendentals=2 * count
        ),
        name="adam_part",
    )(*operands)


def serve_piece(tokens, resident, deltas, place, width):
    rows_total, depth = tokens.shape
    n_parts = len(deltas)
    part_rows = deltas[0].shape[0]
    n_cols = deltas[0].shape[1] // width
    tile = 256 if rows_total % 256 == 0 else rows_total

    def kernel(tab, tok, *refs):
        residents = refs[:n_cols]
        parts = refs[n_cols : n_cols + n_parts * n_cols]
        out, weight = refs[-2:]
        for h in range(n_parts):

            @pl.loop(0, part_rows // QB)
            def _(b):
                at = pl.multiple_of(h * part_rows + b * QB, QB)
                near = pl.multiple_of(b * QB, QB)
                for k in range(n_cols):
                    for c in range(width // QB):
                        span = slice(c * QB, (c + 1) * QB)
                        value = residents[k][pl.ds(at, QB), span].astype(jnp.float32) + parts[
                            h * n_cols + k
                        ][pl.ds(near, QB), span].astype(jnp.float32)
                        largest = jnp.max(jnp.abs(value), axis=(0, 1), keepdims=True)
                        scale = (largest + scale_epsilon) / quant_range
                        level = jnp.floor(value * (1.0 / (scale * grid_step)) + 0.5)
                        weight[pl.ds(at, QB), k * width + c * QB : k * width + (c + 1) * QB] = (
                            level * (scale * grid_step)
                        ).astype(jnp.bfloat16)

        @pl.loop(0, rows_total // tile)
        def _(m):
            at = pl.multiple_of(m * tile, tile)
            product = jnp.dot(
                tok[pl.ds(at, tile), :], weight[...], preferred_element_type=jnp.float32
            )
            for k in range(n_cols):
                out[k, pl.ds(at, tile), :] = product[:, k * width : (k + 1) * width].astype(
                    jnp.bfloat16
                )

    def res_map(k):
        return lambda i, tab: (0, tab[k])

    def delta_map(k):
        return lambda i, tab: (0, tab[n_cols + k])

    in_specs = [pl.BlockSpec((rows_total, depth), lambda i, tab: (0, 0))]
    in_specs += [pl.BlockSpec((depth, width), res_map(k)) for k in range(n_cols)]
    operands = [tokens] + [resident] * n_cols
    for h in range(n_parts):
        for k in range(n_cols):
            in_specs.append(pl.BlockSpec((part_rows, width), delta_map(k)))
            operands.append(deltas[h])
    return pl.pallas_call(
        kernel,
        grid_spec=pltpu.PrefetchScalarGridSpec(
            num_scalar_prefetch=1,
            grid=(1,),
            in_specs=in_specs,
            out_specs=pl.BlockSpec((n_cols, rows_total, width), lambda i, tab: (0, 0, 0)),
            scratch_shapes=[pltpu.VMEM((depth, n_cols * width), jnp.bfloat16)],
        ),
        out_shape=jax.ShapeDtypeStruct((n_cols, rows_total, width), jnp.bfloat16),
        compiler_params=params(),
        cost_estimate=pl.CostEstimate(
            flops=2 * rows_total * depth * n_cols * width,
            bytes_accessed=2 * depth * (rows_total + 2 * n_cols * width),
            transcendentals=0,
        ),
        name="serve_piece",
    )(place, *operands)


def body(
    grad_partials,
    master_weights,
    first_moment,
    second_moment,
    resident_weights,
    token_tiles,
    owner_expert,
    live_rows,
):
    n_dp = lax.axis_size("dp")
    n_expert = lax.axis_size("expert")
    group = n_expert // EXPERTS
    me = lax.axis_index("dp")
    own = lax.axis_index("expert")
    plane = own // group
    lane = own % group
    levels = n_dp.bit_length() - 1
    assert 1 << levels == n_dp and EXPERTS * group == n_expert

    rows, piece_cols = master_weights.shape
    owner_cols = resident_weights.shape[1]
    dp_cols = owner_cols // n_dp
    n_cols = piece_cols // dp_cols
    assert n_cols in (1, 2) and n_cols * dp_cols == piece_cols
    width = QB
    n_chunks = dp_cols // width
    parts = ROW_PARTS if rows % (ROW_PARTS * QB) == 0 else 1
    part_rows = rows // parts
    grad = grad_partials.reshape(n_dp * rows, piece_cols)
    state = (master_weights, first_moment, second_moment)

    def flip(value, level):
        pairs = [(i, i ^ (1 << level)) for i in range(n_dp)]
        return lax.ppermute(value, "dp", pairs)

    def along(value, moves):
        pairs = [(a * group + j, b * group + j) for (a, b) in moves for j in range(group)]
        return lax.ppermute(value, "expert", pairs)

    columns = [[k * dp_cols + c * width for k in range(n_cols)] for c in range(n_chunks)]
    updated_master = None
    delta = [[None] * n_chunks for _ in range(parts)]

    def slab_ids(level):
        relative = jnp.arange(n_dp >> (level + 1), dtype=jnp.int32) * (2 << level) + (1 << level)
        return jnp.bitwise_xor(me.astype(jnp.int32), relative)

    core_recs = []
    for c in range(n_chunks):
        send = slab_sum(grad, slab_ids(0), [], rows, rows, 0, columns[c], width)
        core_recs.append(flip(send, 0))
    mine = me.astype(jnp.int32)[None]
    for c in range(n_chunks):
        for h in range(parts):
            received = [(core_recs[c], h)]
            for level in range(1, levels):
                feed = []
                for j, (array, offset) in enumerate(received):
                    feed.append((array, offset, (1 << level) >> (j + 1), (2 << level) >> (j + 1)))
                send = slab_sum(
                    grad, slab_ids(level), feed, rows, part_rows, h, columns[c], width
                )
                received.append((flip(send, level), 0))
            updated_master, delta[h][c] = adam_part(
                grad, mine, received, state, updated_master, rows, part_rows, h, columns[c], width
            )

    last = EXPERTS - 1
    two_slots = EXPERTS == 4 and group == 2

    def needed(expert, at_plane):
        hosts = owner_expert[at_plane * group : (at_plane + 1) * group]
        return jnp.any(hosts == expert)

    def line(pieces, mirror):
        at = last - plane if mirror else plane
        place = (lambda p: last - p) if mirror else (lambda p: p)
        moves = lambda pairs: [(place(a), place(b)) for a, b in pairs]
        if not two_slots:
            got = []
            for piece in pieces:
                hops, value = [], piece
                for k in range(1, EXPERTS):
                    value = along(value, moves([(p, p + 1) for p in range(k - 1, last)]))
                    hops.append(value)
                got.append(hops)

            def index_of(expert):
                return at - place(expert) - 1

            return got, index_of
        near = needed(place(2), place(3))
        far = needed(place(0), place(3))
        steps = []
        count = len(pieces)
        for t in range(2 * count + 1):
            c = t // 2
            if t % 2:
                value = jnp.where((at == 2) & near, pieces[c], steps[2 * c])
                pairs = [(1, 2), (2, 3)]
            elif t == 0:
                value, pairs = pieces[0], [(0, 1), (1, 2)]
            else:
                value = jnp.where(far, steps[t - 1], steps[t - 2])
                pairs = [(2, 3)]
                if c < count:
                    value = jnp.where(at == 2, value, pieces[c])
                    pairs = [(0, 1), (1, 2), (2, 3)]
            steps.append(along(value, moves(pairs)))
        got = [steps[2 * c : 2 * c + 3] for c in range(count)]

        def index_of(expert):
            seen = place(expert)
            slot = jnp.where(seen == jnp.where(near, 2, 1), 1, 2)
            return jnp.where(at == 3, slot, jnp.where(at == 2, 1 - seen, 0))

        return got, index_of

    def choose(index, options):
        value = options[0]
        for k in range(1, len(options)):
            value = jnp.where(index == k, options[k], value)
        return value

    own_pieces = [[None] * parts for _ in range(n_chunks)]
    moved_pieces = [[[None] * parts for _ in range(n_chunks)] for _ in range(group)]
    streams = []
    for h in range(parts):
        up, up_index = line(delta[h], False)
        down, down_index = line(delta[h], True)
        streams.append((up, up_index, down, down_index))
    for c in range(n_chunks):
        for h in range(parts):
            up, up_index, down, down_index = streams[h]
            for s in range(group):
                target = plane * group + (lane + s) % group
                expert = owner_expert[target]
                value = jnp.where(
                    expert < plane,
                    choose(up_index(expert), up[c]),
                    choose(down_index(expert), down[c]),
                )
                value = jnp.where(expert == plane, delta[h][c], value)
                if s:
                    pairs = [
                        (e * group + j, e * group + (j + s) % group)
                        for e in range(EXPERTS)
                        for j in range(group)
                    ]
                    value = lax.ppermute(value, "expert", pairs)
                moved_pieces[s][c][h] = value

    sums = []
    parity = (me % 2).astype(jnp.int32)
    for c in range(n_chunks):
        products = []
        for s in range(group):
            piece = ((lane - s) % group).astype(jnp.int32)
            order = [k ^ parity for k in range(n_cols)] if n_cols == 2 else [jnp.int32(0)]
            place = jnp.stack(
                [(piece * piece_cols + k * dp_cols + c * width) // width for k in order] + order
            )
            products.append(
                serve_piece(token_tiles, resident_weights, moved_pieces[s][c], place, width)
            )
        if n_dp == 4 and group == 2:
            crossed = flip(jnp.stack([product[1] for product in products]), 0)
            kept = [
                products[s][0].astype(jnp.float32) + crossed[s].astype(jnp.float32)
                for s in range(2)
            ]
            straight = lane == me // 2
            other = jnp.where(straight, kept[1], kept[0]).astype(jnp.bfloat16)
            held = jnp.where(straight, kept[0], kept[1])
            sums.append(held + flip(other, 1).astype(jnp.float32))
        else:
            buffer = jnp.zeros((n_dp,) + products[0].shape[1:], jnp.bfloat16)
            for s in range(group):
                piece = (lane - s) % group
                for k in range(n_cols):
                    column = piece * n_cols + ((k ^ parity) if n_cols == 2 else 0)
                    buffer = lax.dynamic_update_index_in_dim(
                        buffer, products[s][k], jnp.bitwise_xor(column, me), 0
                    )
            for level in range(levels):
                got = flip(buffer[1::2], level).astype(jnp.float32)
                buffer = (buffer[0::2].astype(jnp.float32) + got).astype(
                    jnp.bfloat16 if level < levels - 1 else jnp.float32
                )
            sums.append(buffer[0])
    summed = jnp.concatenate(sums, axis=1)
    row_index = lax.broadcasted_iota(jnp.int32, summed.shape, 0)
    projected = jnp.where(row_index < live_rows[0], summed, jnp.float32(0.0)).astype(jnp.bfloat16)
    return (updated_master, projected)


def solution(mesh):
    placed = (
        P("dp", None, "expert"),
        P("dp", "expert"),
        P("dp", "expert"),
        P("dp", "expert"),
        P("dp", "expert"),
        P("expert", "dp"),
        P(),
        P("expert"),
    )
    return jax.shard_map(
        body,
        mesh=mesh,
        in_specs=placed,
        out_specs=(P("dp", "expert"), P("expert", "dp")),
        check_vma=False,
    )
```

```python
import jax
import jax.numpy as jnp
from jax import lax
from jax.experimental import pallas as pl
from jax.experimental.pallas import tpu as pltpu
from jax.sharding import PartitionSpec as P


EXPERTS = 4
QB = 128

beta_first = 0.9
beta_second = 0.95
learn_rate = 0.02
decay_rate = 0.1
adam_epsilon = 1e-08
scale_epsilon = 1e-06
quant_range = 448.0
grid_step = 8.0
bias_first = 1.0 - 0.9**20
bias_second = 1.0 - 0.95**20

ROW_PARTS = 2
TILE = 1024
UNROLL = 7
ADAM_SPLIT = 1
SUM_VMEM = 50 << 20
PICK_VMEM = 16 << 20
ADAM_VMEM = 58 << 20
SERVE_VMEM = 50 << 20


def adamw(gradient, master_weights, first_moment, second_moment):
    moment_one = beta_first * first_moment + (1.0 - beta_first) * gradient
    moment_two = beta_second * second_moment + (1.0 - beta_second) * gradient * gradient
    update = (moment_one * (1.0 / bias_first)) / (
        jnp.sqrt(moment_two * (1.0 / bias_second)) + adam_epsilon
    )
    return master_weights - learn_rate * (update + decay_rate * master_weights)


def params(limit):
    return pltpu.CompilerParams(vmem_limit_bytes=limit)


def total(refs):
    value = refs[0].astype(jnp.float32)
    for ref in refs[1:]:
        value = value + ref.astype(jnp.float32)
    return value


def slab_sum(grad, table, relative, received, rows, part_rows, part, cols, width):
    n_out = len(relative)
    skip = relative[1] - relative[0] if n_out > 1 else 0
    n_cols = len(cols)
    block = part_rows
    step = rows // block
    n_rows = part_rows // block

    def kernel(tab, *refs):
        grads, recs, out = refs[:n_cols], refs[n_cols:-1], refs[-1]
        for k in range(n_cols):
            span = slice(k * width, (k + 1) * width)
            values = [grads[k][...]] + [rec[0, :, span] for rec in recs]
            out[0, :, span] = total(values).astype(out.dtype)

    def grad_map(k):
        at = cols[k] // width
        return lambda i, r, tab: (tab[relative[0] + i * skip] * step + part * n_rows + r, at)

    def rec_map(stride, offset, first):
        return lambda i, r, tab: (first + i * stride, offset * n_rows + r, 0)

    in_specs = [pl.BlockSpec((block, width), grad_map(k)) for k in range(n_cols)]
    in_specs += [
        pl.BlockSpec((1, block, n_cols * width), rec_map(stride, offset, first))
        for (_, offset, first, stride) in received
    ]
    moved = n_out * part_rows * n_cols * width * 2
    return pl.pallas_call(
        kernel,
        grid_spec=pltpu.PrefetchScalarGridSpec(
            num_scalar_prefetch=1,
            grid=(n_out, n_rows),
            in_specs=in_specs,
            out_specs=pl.BlockSpec((1, block, n_cols * width), lambda i, r, tab: (i, r, 0)),
        ),
        out_shape=jax.ShapeDtypeStruct((n_out, part_rows, n_cols * width), jnp.bfloat16),
        compiler_params=params(SUM_VMEM),
        cost_estimate=pl.CostEstimate(
            flops=moved, bytes_accessed=moved * (2 + len(received)), transcendentals=0
        ),
        name="slab_sum",
    )(table, *([grad] * n_cols), *[item[0] for item in received])


def adam_part(grad, table, received, state, out, rows, part_rows, part, cols, width):
    n_cols = len(cols)
    block = part_rows // ADAM_SPLIT if part_rows % (ADAM_SPLIT * 16) == 0 else part_rows
    step = rows // block
    n_rows = part_rows // block
    base = cols[0] // width
    stride = (cols[1] - cols[0]) // width if n_cols > 1 else 0
    n_rec = len(received)

    def kernel(tab, grad_ref, *refs):
        recs = refs[:n_rec]
        master, first, second = refs[n_rec : n_rec + 3]
        new_ref, delta_ref = refs[-2:]
        gradient = total([grad_ref[...]] + [rec[0] for rec in recs])
        old = master[...]
        new = adamw(gradient, old, first[...], second[...])
        new_ref[...] = new
        delta_ref[...] = (new - old).astype(delta_ref.dtype)

    def state_map(r, k, tab):
        return (part * n_rows + r, base + k * stride)

    state_spec = pl.BlockSpec((block, width), state_map)
    in_specs = [
        pl.BlockSpec(
            (block, width), lambda r, k, tab: (tab[0] * step + part * n_rows + r, base + k * stride)
        )
    ]

    def rec_map(offset):
        return lambda r, k, tab: (0, offset * n_rows + r, k)

    in_specs += [pl.BlockSpec((1, block, width), rec_map(offset)) for (_, offset) in received]
    in_specs += [state_spec] * 3
    operands = [table, grad, *[item[0] for item in received], *state]
    aliases = {}
    if out is not None:
        in_specs.append(pl.BlockSpec(memory_space=pl.ANY))
        aliases = {len(operands): 0}
        operands.append(out)
    count = part_rows * n_cols * width
    return pl.pallas_call(
        kernel,
        grid_spec=pltpu.PrefetchScalarGridSpec(
            num_scalar_prefetch=1,
            grid=(n_rows, n_cols),
            in_specs=in_specs,
            out_specs=(
                state_spec,
                pl.BlockSpec((block, width), lambda r, k, tab: (r, k)),
            ),
        ),
        out_shape=(
            jax.ShapeDtypeStruct(state[0].shape, jnp.float32),
            jax.ShapeDtypeStruct((part_rows, n_cols * width), jnp.bfloat16),
        ),
        input_output_aliases=aliases,
        compiler_params=params(ADAM_VMEM),
        cost_estimate=pl.CostEstimate(
            flops=30 * count, bytes_accessed=(20 + 2 * n_rec) * count, transcendentals=2 * count
        ),
        name="adam_part",
    )(*operands)


def pick(table, code_of, options):
    shape = options[0].shape

    def kernel(tab, *refs):
        out, sem = refs[-2:]
        code = code_of(tab)
        for k in range(len(options)):

            @pl.when(code == k)
            def _():
                copy = pltpu.make_async_copy(refs[k], out, sem)
                copy.start()
                copy.wait()

    return pl.pallas_call(
        kernel,
        grid_spec=pltpu.PrefetchScalarGridSpec(
            num_scalar_prefetch=1,
            grid=(1,),
            in_specs=[pl.BlockSpec(memory_space=pl.ANY)] * len(options),
            out_specs=pl.BlockSpec(shape, lambda i, tab: (0, 0)),
            scratch_shapes=[pltpu.SemaphoreType.DMA],
        ),
        out_shape=jax.ShapeDtypeStruct(shape, options[0].dtype),
        compiler_params=params(PICK_VMEM),
        cost_estimate=pl.CostEstimate(
            flops=0, bytes_accessed=4 * shape[0] * shape[1], transcendentals=0
        ),
        name="pick",
    )(table, *options)


def serve_piece(tokens, resident, parts, code_of, table, places, stride, shift, width):
    rows_total, depth = tokens.shape
    n_parts = len(parts)
    n_options = len(parts[0])
    part_rows, part_cols = parts[0][0].shape
    n_cols = part_cols // width
    tile = TILE if rows_total % TILE == 0 else rows_total

    def kernel(tab, tok, *refs):
        residents = refs[:n_cols]
        options = refs[n_cols : n_cols + n_parts * n_options]
        out, weight, delta, sems = refs[-4:]
        code = code_of(tab)
        for k in range(n_options):

            @pl.when(code == k)
            def _():
                copies = [
                    pltpu.make_async_copy(options[h * n_options + k], delta.at[h], sems.at[h])
                    for h in range(n_parts)
                ]
                for copy in copies:
                    copy.start()
                for copy in copies:
                    copy.wait()

        starts = [
            pl.multiple_of(lax.rem(tab[places[k]], n_cols) * width, width) for k in range(n_cols)
        ]
        for h in range(n_parts):

            @pl.loop(0, part_rows // QB, unroll=UNROLL)
            def _(b):
                at = pl.multiple_of(h * part_rows + b * QB, QB)
                near = pl.multiple_of(b * QB, QB)
                for k in range(n_cols):
                    for c in range(width // QB):
                        span = slice(c * QB, (c + 1) * QB)
                        change = delta[h, pl.ds(near, QB), pl.ds(starts[k] + c * QB, QB)]
                        value = residents[k][pl.ds(at, QB), span].astype(
                            jnp.float32
                        ) + change.astype(jnp.float32)
                        largest = jnp.max(jnp.abs(value), axis=(0, 1), keepdims=True)
                        scale = (largest + scale_epsilon) / quant_range
                        level = jnp.floor(value * (1.0 / (scale * grid_step)) + 0.5)
                        weight[pl.ds(at, QB), k * width + c * QB : k * width + (c + 1) * QB] = (
                            level * (scale * grid_step)
                        ).astype(jnp.bfloat16)

        @pl.loop(0, rows_total // tile)
        def _(m):
            at = pl.multiple_of(m * tile, tile)
            product = jnp.dot(
                tok[pl.ds(at, tile), :], weight[...], preferred_element_type=jnp.float32
            )
            for k in range(n_cols):
                out[k, pl.ds(at, tile), :] = product[:, k * width : (k + 1) * width].astype(
                    jnp.bfloat16
                )

    def res_map(k):
        return lambda i, tab: (0, tab[places[k]] * stride + shift)

    in_specs = [pl.BlockSpec((rows_total, depth), lambda i, tab: (0, 0))]
    in_specs += [pl.BlockSpec((depth, width), res_map(k)) for k in range(n_cols)]
    in_specs += [pl.BlockSpec(memory_space=pl.ANY)] * (n_parts * n_options)
    operands = [tokens] + [resident] * n_cols + [option for part in parts for option in part]
    return pl.pallas_call(
        kernel,
        grid_spec=pltpu.PrefetchScalarGridSpec(
            num_scalar_prefetch=1,
            grid=(1,),
            in_specs=in_specs,
            out_specs=pl.BlockSpec((n_cols, rows_total, width), lambda i, tab: (0, 0, 0)),
            scratch_shapes=[
                pltpu.VMEM((depth, n_cols * width), jnp.bfloat16),
                pltpu.VMEM((n_parts, part_rows, part_cols), jnp.bfloat16),
                pltpu.SemaphoreType.DMA((n_parts,)),
            ],
        ),
        out_shape=jax.ShapeDtypeStruct((n_cols, rows_total, width), jnp.bfloat16),
        compiler_params=params(SERVE_VMEM),
        cost_estimate=pl.CostEstimate(
            flops=2 * rows_total * depth * n_cols * width,
            bytes_accessed=2 * depth * (rows_total + 2 * n_cols * width),
            transcendentals=0,
        ),
        name="serve_piece",
    )(table, *operands)


def make_table(me, own, owner_expert, n_dp, group, n_cols, two_slots):
    place_at = n_dp
    code_at = place_at + group * n_cols
    flag_at = code_at + group
    last = EXPERTS - 1

    def kernel(here, hosts, out):
        me = here[0]
        plane = lax.div(here[1], group)
        lane = lax.rem(here[1], group)
        for r in range(n_dp):
            out[r] = jnp.bitwise_xor(me, r)
        for s in range(group):
            piece = lax.rem(lane + group - s, group)
            for k in range(n_cols):
                column = jnp.bitwise_xor(jnp.bitwise_and(me, n_cols - 1), k)
                out[place_at + s * n_cols + k] = piece * n_cols + column
        outer = jnp.where(plane < EXPERTS // 2, 0, last)
        inner = jnp.where(plane < EXPERTS // 2, 1, last - 1)
        near = jnp.int32(0)
        far = jnp.int32(0)
        for j in range(group):
            host = hosts[outer * group + j]
            near = jnp.where(host == inner, 1, near)
            far = jnp.where(host == last - outer, 1, far)
        at_end = jnp.where(plane == outer, 1, 0)
        for s in range(group):
            expert = hosts[plane * group + lax.rem(lane + s, group)]
            if two_slots:
                first = jnp.where(near == 1, inner, last - inner)
                code_end = jnp.where(expert == first, 2, 3)
                code_mid = jnp.where(expert == outer, 1, jnp.where(expert == last - plane, 4, 5))
                code = jnp.where(at_end == 1, code_end, code_mid)
            else:
                code = jnp.where(expert < plane, plane - expert, last + expert - plane)
            out[code_at + s] = jnp.where(expert == plane, 0, code)
        out[flag_at] = near
        out[flag_at + 1] = far
        out[flag_at + 2] = at_end
        out[flag_at + 3] = jnp.where(lane == lax.div(me, 2), 1, 0)

    table = pl.pallas_call(
        kernel,
        in_specs=[pl.BlockSpec(memory_space=pltpu.SMEM)] * 2,
        out_specs=pl.BlockSpec(memory_space=pltpu.SMEM),
        out_shape=jax.ShapeDtypeStruct((flag_at + 4,), jnp.int32),
        name="make_table",
    )(jnp.stack([me, own]).astype(jnp.int32), owner_expert)
    return table, place_at, code_at, flag_at


def body(
    grad_partials,
    master_weights,
    first_moment,
    second_moment,
    resident_weights,
    token_tiles,
    owner_expert,
    live_rows,
):
    n_dp = lax.axis_size("dp")
    n_expert = lax.axis_size("expert")
    group = n_expert // EXPERTS
    me = lax.axis_index("dp")
    own = lax.axis_index("expert")
    lane = own % group
    levels = n_dp.bit_length() - 1
    assert 1 << levels == n_dp and EXPERTS * group == n_expert

    rows, piece_cols = master_weights.shape
    owner_cols = resident_weights.shape[1]
    dp_cols = owner_cols // n_dp
    n_cols = piece_cols // dp_cols
    assert n_cols in (1, 2) and n_cols * dp_cols == piece_cols
    width = QB
    n_chunks = dp_cols // width
    parts = ROW_PARTS if rows % (ROW_PARTS * QB) == 0 else 1
    part_rows = rows // parts
    grad = grad_partials.reshape(n_dp * rows, piece_cols)
    state = (master_weights, first_moment, second_moment)

    two_slots = EXPERTS == 4 and group == 2
    table, place_at, code_at, flag_at = make_table(
        me, own, owner_expert, n_dp, group, n_cols, two_slots
    )

    def flip(value, level):
        pairs = [(i, i ^ (1 << level)) for i in range(n_dp)]
        return lax.ppermute(value, "dp", pairs)

    def along(value, moves):
        pairs = [(a * group + j, b * group + j) for (a, b) in moves for j in range(group)]
        return lax.ppermute(value, "expert", pairs)

    columns = [[k * dp_cols + c * width for k in range(n_cols)] for c in range(n_chunks)]
    updated_master = None
    delta = [[None] * n_chunks for _ in range(parts)]

    def relative(level):
        return [(1 << level) + i * (2 << level) for i in range(n_dp >> (level + 1))]

    core_recs = []
    for c in range(n_chunks):
        send = slab_sum(grad, table, relative(0), [], rows, rows, 0, columns[c], width)
        core_recs.append(flip(send, 0))
    for c in range(n_chunks):
        for h in range(parts):
            received = [(core_recs[c], h)]
            for level in range(1, levels):
                feed = []
                for j, (array, offset) in enumerate(received):
                    feed.append((array, offset, (1 << level) >> (j + 1), (2 << level) >> (j + 1)))
                send = slab_sum(
                    grad, table, relative(level), feed, rows, part_rows, h, columns[c], width
                )
                received.append((flip(send, level), 0))
            updated_master, delta[h][c] = adam_part(
                grad,
                table,
                received,
                state,
                updated_master,
                rows,
                part_rows,
                h,
                columns[c],
                width,
            )

    last = EXPERTS - 1

    def at(index):
        return lambda tab: tab[index]

    def full_line(pieces):
        found = []
        for piece in pieces:
            options = [piece]
            for side in range(2):
                value = piece
                for k in range(1, EXPERTS):
                    moves = [(p, p + 1) for p in range(k - 1, last)]
                    if side:
                        moves = [(last - a, last - b) for a, b in moves]
                    value = along(value, moves)
                    options.append(value)
            found.append(options)
        return found

    def slotted_line(pieces):
        sides = [(0, 1), (1, 0), (2, 3), (3, 2)]
        middle = [(1, 2), (2, 1)]
        count = len(pieces)
        side, center = [], []

        def odd_code(tab):
            return 1 - tab[flag_at]

        def even_code(tab):
            return jnp.where(tab[flag_at + 2] == 1, 2, tab[flag_at + 1])

        def last_code(tab):
            return tab[flag_at + 1]

        for t in range(2 * count + 1):
            c = t // 2
            if t == 0:
                value = pieces[0]
            else:
                if t % 2:
                    value = pick(table, odd_code, [pieces[c], center[2 * c]])
                elif c < count:
                    value = pick(table, even_code, [center[t - 2], center[t - 1], pieces[c]])
                else:
                    value = pick(table, last_code, [center[t - 2], center[t - 1]])
            side.append(along(value, sides))
            if t < 2 * count:
                center.append(along(side[t - 1] if t % 2 else pieces[c], middle))
        return [
            [pieces[c], *side[2 * c : 2 * c + 3], *center[2 * c : 2 * c + 2]] for c in range(count)
        ]

    if two_slots:
        options = [slotted_line(delta[h]) for h in range(parts)]
    else:
        options = [full_line(delta[h]) for h in range(parts)]

    moved = [[[None] * parts for _ in range(n_chunks)] for _ in range(group)]
    for c in range(n_chunks):
        for h in range(parts):
            for s in range(1, group):
                value = pick(table, at(code_at + s), options[h][c])
                pairs = [
                    (e * group + j, e * group + (j + s) % group)
                    for e in range(EXPERTS)
                    for j in range(group)
                ]
                moved[s][c][h] = lax.ppermute(value, "expert", pairs)

    sums = []
    parity = (me % 2).astype(jnp.int32)
    for c in range(n_chunks):
        products = []
        for s in range(group):
            if s == 0:
                sources, code_of = [options[h][c] for h in range(parts)], at(code_at)
            else:
                sources, code_of = [[moved[s][c][h]] for h in range(parts)], lambda tab: 0
            products.append(
                serve_piece(
                    token_tiles,
                    resident_weights,
                    sources,
                    code_of,
                    table,
                    [place_at + s * n_cols + k for k in range(n_cols)],
                    n_chunks,
                    c,
                    width,
                )
            )
        if n_dp == 4 and group == 2:
            stacked = jnp.stack([product[1] for product in products])
            crossed = flip(stacked, 0)
            kept = [
                products[s][0].astype(jnp.float32) + crossed[s].astype(jnp.float32)
                for s in range(2)
            ]
            straight = table[flag_at + 3] == 1
            other = jnp.where(straight, kept[1], kept[0]).astype(jnp.bfloat16)
            held = jnp.where(straight, kept[0], kept[1])
            crossed = flip(other, 1)
            sums.append(held + crossed.astype(jnp.float32))
        else:
            buffer = jnp.zeros((n_dp,) + products[0].shape[1:], jnp.bfloat16)
            for s in range(group):
                piece = (lane - s) % group
                for k in range(n_cols):
                    column = piece * n_cols + ((k ^ parity) if n_cols == 2 else 0)
                    buffer = lax.dynamic_update_index_in_dim(
                        buffer, products[s][k], jnp.bitwise_xor(column, me), 0
                    )
            for level in range(levels):
                got = flip(buffer[1::2], level).astype(jnp.float32)
                buffer = (buffer[0::2].astype(jnp.float32) + got).astype(
                    jnp.bfloat16 if level < levels - 1 else jnp.float32
                )
            sums.append(buffer[0])
    summed = jnp.concatenate(sums, axis=1)
    row_index = lax.broadcasted_iota(jnp.int32, summed.shape, 0)
    projected = jnp.where(row_index < live_rows[0], summed, jnp.float32(0.0)).astype(jnp.bfloat16)
    return (updated_master, projected)


def solution(mesh):
    placed = (
        P("dp", None, "expert"),
        P("dp", "expert"),
        P("dp", "expert"),
        P("dp", "expert"),
        P("dp", "expert"),
        P("expert", "dp"),
        P(),
        P("expert"),
    )

    return jax.shard_map(
        body,
        mesh=mesh,
        in_specs=placed,
        out_specs=(P("dp", "expert"), P("expert", "dp")),
        check_vma=False,
    )
```

```python
import jax
import jax.numpy as jnp
from jax import lax
from jax.experimental import pallas as pl
from jax.experimental.pallas import tpu as pltpu
from jax.sharding import PartitionSpec as P


EXPERTS = 4
QB = 128

beta_first = 0.9
beta_second = 0.95
learn_rate = 0.02
decay_rate = 0.1
adam_epsilon = 1e-08
scale_epsilon = 1e-06
quant_range = 448.0
grid_step = 8.0
bias_first = 1.0 - 0.9**20
bias_second = 1.0 - 0.95**20

ROW_PARTS = 2
TILE = 1024
UNROLL = 7
SUM_VMEM = 50 << 20
PICK_VMEM = 16 << 20
ADAM_VMEM = 57 << 20
SERVE_VMEM = 50 << 20


def adamw(gradient, master_weights, first_moment, second_moment):
    moment_one = beta_first * first_moment + (1.0 - beta_first) * gradient
    moment_two = beta_second * second_moment + (1.0 - beta_second) * gradient * gradient
    update = (moment_one * (1.0 / bias_first)) / (
        jnp.sqrt(moment_two * (1.0 / bias_second)) + adam_epsilon
    )
    return master_weights - learn_rate * (update + decay_rate * master_weights)


def params(limit):
    return pltpu.CompilerParams(vmem_limit_bytes=limit)


def total(refs):
    value = refs[0].astype(jnp.float32)
    for ref in refs[1:]:
        value = value + ref.astype(jnp.float32)
    return value


def slab_sum(grad, table, relative, received, rows, part_rows, part, cols, width):
    n_out = len(relative)
    skip = relative[1] - relative[0] if n_out > 1 else 0
    n_cols = len(cols)
    block = part_rows
    step = rows // block
    n_rows = part_rows // block

    def kernel(tab, *refs):
        grads, recs, out = refs[:n_cols], refs[n_cols:-1], refs[-1]
        for k in range(n_cols):
            span = slice(k * width, (k + 1) * width)
            values = [grads[k][...]] + [rec[0, :, span] for rec in recs]
            out[0, :, span] = total(values).astype(out.dtype)

    def grad_map(k):
        at = cols[k] // width
        return lambda i, r, tab: (jnp.bitwise_xor(tab[0], relative[0] + i * skip) * step + part * n_rows + r, at)

    def rec_map(stride, offset, first):
        return lambda i, r, tab: (first + i * stride, offset * n_rows + r, 0)

    in_specs = [pl.BlockSpec((block, width), grad_map(k)) for k in range(n_cols)]
    in_specs += [
        pl.BlockSpec((1, block, n_cols * width), rec_map(stride, offset, first))
        for (_, offset, first, stride) in received
    ]
    moved = n_out * part_rows * n_cols * width * 2
    return pl.pallas_call(
        kernel,
        grid_spec=pltpu.PrefetchScalarGridSpec(
            num_scalar_prefetch=1,
            grid=(n_out, n_rows),
            in_specs=in_specs,
            out_specs=pl.BlockSpec((1, block, n_cols * width), lambda i, r, tab: (i, r, 0)),
        ),
        out_shape=jax.ShapeDtypeStruct((n_out, part_rows, n_cols * width), jnp.bfloat16),
        compiler_params=params(SUM_VMEM),
        cost_estimate=pl.CostEstimate(
            flops=moved, bytes_accessed=moved * (2 + len(received)), transcendentals=0
        ),
        name="slab_sum",
    )(table, *([grad] * n_cols), *[item[0] for item in received])


def adam_parts(grad, table, received, state, out, rows, part_rows, parts, cols, width):
    n_cols = len(cols)
    block = part_rows
    step = rows // block
    n_parts = len(parts)
    first_part = parts[0]
    base = cols[0] // width
    stride = (cols[1] - cols[0]) // width if n_cols > 1 else 0
    n_rec = len(received)

    def kernel(tab, grad_ref, *refs):
        recs = refs[:n_rec]
        master, first, second = refs[n_rec : n_rec + 3]
        new_ref = refs[-1 - n_parts]
        deltas = refs[-n_parts:]
        gradient = total([grad_ref[...]] + [rec[0] for rec in recs])
        old = master[...]
        new = adamw(gradient, old, first[...], second[...])
        new_ref[...] = new
        change = (new - old).astype(jnp.bfloat16)
        if n_parts == 1:
            deltas[0][...] = change
        else:
            for h in range(n_parts):

                @pl.when(pl.program_id(0) == h)
                def _():
                    deltas[h][...] = change

    def state_map(r, k, tab):
        return (first_part + r, base + k * stride)

    state_spec = pl.BlockSpec((block, width), state_map)
    in_specs = [
        pl.BlockSpec((block, width), lambda r, k, tab: (tab[0] * step + first_part + r, base + k * stride))
    ]

    def rec_map(offset):
        return lambda r, k, tab: (0, offset + r, k)

    def delta_map(h):
        return lambda r, k, tab: (0, jnp.where(r == h, k, jnp.where(r < h, 0, n_cols - 1)))

    in_specs += [pl.BlockSpec((1, block, width), rec_map(offset)) for (_, offset) in received]
    in_specs += [state_spec] * 3
    operands = [table, grad, *[item[0] for item in received], *state]
    aliases = {}
    if out is not None:
        in_specs.append(pl.BlockSpec(memory_space=pl.ANY))
        aliases = {len(operands): 0}
        operands.append(out)
    count = n_parts * part_rows * n_cols * width
    result = pl.pallas_call(
        kernel,
        grid_spec=pltpu.PrefetchScalarGridSpec(
            num_scalar_prefetch=1,
            grid=(n_parts, n_cols),
            in_specs=in_specs,
            out_specs=(
                state_spec,
                *[pl.BlockSpec((block, width), delta_map(h)) for h in range(n_parts)],
            ),
        ),
        out_shape=(
            jax.ShapeDtypeStruct(state[0].shape, jnp.float32),
            *[jax.ShapeDtypeStruct((part_rows, n_cols * width), jnp.bfloat16)] * n_parts,
        ),
        input_output_aliases=aliases,
        compiler_params=params(ADAM_VMEM),
        cost_estimate=pl.CostEstimate(
            flops=30 * count, bytes_accessed=(20 + 2 * n_rec) * count, transcendentals=2 * count
        ),
        name="adam_parts",
    )(*operands)
    return result[0], result[1:]


def pick(table, code_of, parts):
    part_rows, cols = parts[0][0].shape
    n_parts, n_options = len(parts), len(parts[0])
    shape = (n_parts * part_rows, cols)

    def kernel(tab, *refs):
        out, sems = refs[-2:]
        code = code_of(tab)
        for k in range(n_options):

            @pl.when(code == k)
            def _():
                copies = [
                    pltpu.make_async_copy(
                        refs[h * n_options + k], out.at[pl.ds(h * part_rows, part_rows)], sems.at[h]
                    )
                    for h in range(n_parts)
                ]
                for copy in copies:
                    copy.start()
                for copy in copies:
                    copy.wait()

    return pl.pallas_call(
        kernel,
        grid_spec=pltpu.PrefetchScalarGridSpec(
            num_scalar_prefetch=1,
            grid=(1,),
            in_specs=[pl.BlockSpec(memory_space=pl.ANY)] * (n_parts * n_options),
            out_specs=pl.BlockSpec(shape, lambda i, tab: (0, 0)),
            scratch_shapes=[pltpu.SemaphoreType.DMA((n_parts,))],
        ),
        out_shape=jax.ShapeDtypeStruct(shape, parts[0][0].dtype),
        compiler_params=params(PICK_VMEM),
        cost_estimate=pl.CostEstimate(
            flops=0, bytes_accessed=4 * shape[0] * shape[1], transcendentals=0
        ),
        name="pick",
    )(table, *[option for options in parts for option in options])


def serve(tokens, resident, pieces, table, part_rows, stride, shift, width):
    rows_total, depth = tokens.shape
    n_pieces = len(pieces)
    n_parts = len(pieces[0][0])
    part_cols = pieces[0][0][0][0][0].shape[1]
    n_cols = part_cols // width
    tile = TILE if rows_total % TILE == 0 else rows_total
    counts = [len(parts[0]) for parts, _, _ in pieces]

    def kernel(tab, tokens_ref, resident_ref, *refs):
        outs = refs[-7 - n_cols : -7]
        tok, held, weight, delta, sems, held_sems, tok_sem = refs[-7:]
        at_ref = 0

        def fetch_resident(s, k):
            column = (tab[pieces[s][2][k]] * stride + shift) * width
            return pltpu.make_async_copy(
                resident_ref.at[:, pl.ds(pl.multiple_of(column, width), width)],
                held.at[s, k],
                held_sems.at[s, k],
            )

        fetch_tokens = pltpu.make_async_copy(tokens_ref, tok, tok_sem)

        def fetch(s, h, ref):
            return pltpu.make_async_copy(ref, delta.at[s, h], sems.at[s, h])

        for s, (parts, code_of, _) in enumerate(pieces):
            code = code_of(tab)
            for k in range(counts[s]):
                chosen = [
                    refs[at_ref + h * counts[s] + k].at[pl.ds(parts[h][k][1], part_rows)]
                    for h in range(n_parts)
                ]

                @pl.when(code == k)
                def _():
                    for h in range(n_parts):
                        fetch(s, h, chosen[h]).start()

            at_ref += n_parts * counts[s]
            for k in range(n_cols):
                fetch_resident(s, k).start()
        fetch_tokens.start()
        for s, (_, _, places) in enumerate(pieces):
            starts = [
                pl.multiple_of(lax.rem(tab[places[k]], n_cols) * width, width)
                for k in range(n_cols)
            ]
            for k in range(n_cols):
                fetch_resident(s, k).wait()
            for h in range(n_parts):
                fetch(s, h, delta.at[s, h]).wait()

                @pl.loop(0, part_rows // QB, unroll=UNROLL)
                def _(b):
                    at = pl.multiple_of(h * part_rows + b * QB, QB)
                    near = pl.multiple_of(b * QB, QB)
                    for k in range(n_cols):
                        for c in range(width // QB):
                            span = slice(c * QB, (c + 1) * QB)
                            change = delta[s, h, pl.ds(near, QB), pl.ds(starts[k] + c * QB, QB)]
                            value = held[s, k, pl.ds(at, QB), span].astype(
                                jnp.float32
                            ) + change.astype(jnp.float32)
                            largest = jnp.max(jnp.abs(value), axis=(0, 1), keepdims=True)
                            scale = (largest + scale_epsilon) / quant_range
                            level = jnp.floor(value * (1.0 / (scale * grid_step)) + 0.5)
                            column = (s * n_cols + k) * width + c * QB
                            weight[pl.ds(at, QB), column : column + QB] = (
                                level * (scale * grid_step)
                            ).astype(jnp.bfloat16)

        fetch_tokens.wait()

        @pl.loop(0, rows_total // tile)
        def _(m):
            at = pl.multiple_of(m * tile, tile)
            product = jnp.dot(
                tok[pl.ds(at, tile), :], weight[...], preferred_element_type=jnp.float32
            )
            for s in range(n_pieces):
                for k in range(n_cols):
                    column = (s * n_cols + k) * width
                    outs[k][s, pl.ds(at, tile), :] = product[:, column : column + width].astype(
                        jnp.bfloat16
                    )

    in_specs = [pl.BlockSpec(memory_space=pl.ANY)] * 2
    operands = [tokens, resident]
    for parts, _, _ in pieces:
        for options in parts:
            in_specs += [pl.BlockSpec(memory_space=pl.ANY)] * len(options)
            operands += [array for array, _ in options]
    out_spec = pl.BlockSpec((n_pieces, rows_total, width), lambda i, tab: (0, 0, 0))
    out_shape = jax.ShapeDtypeStruct((n_pieces, rows_total, width), jnp.bfloat16)
    return pl.pallas_call(
        kernel,
        grid_spec=pltpu.PrefetchScalarGridSpec(
            num_scalar_prefetch=1,
            grid=(1,),
            in_specs=in_specs,
            out_specs=(out_spec,) * n_cols,
            scratch_shapes=[
                pltpu.VMEM((rows_total, depth), jnp.bfloat16),
                pltpu.VMEM((n_pieces, n_cols, depth, width), jnp.bfloat16),
                pltpu.VMEM((depth, n_pieces * n_cols * width), jnp.bfloat16),
                pltpu.VMEM((n_pieces, n_parts, part_rows, part_cols), jnp.bfloat16),
                pltpu.SemaphoreType.DMA((n_pieces, n_parts)),
                pltpu.SemaphoreType.DMA((n_pieces, n_cols)),
                pltpu.SemaphoreType.DMA,
            ],
        ),
        out_shape=(out_shape,) * n_cols,
        compiler_params=params(SERVE_VMEM),
        cost_estimate=pl.CostEstimate(
            flops=2 * rows_total * depth * n_pieces * n_cols * width,
            bytes_accessed=2 * depth * (rows_total + 2 * n_pieces * n_cols * width),
            transcendentals=0,
        ),
        name="serve",
    )(table, *operands)


def make_table(here, owner_expert, group, n_cols, two_slots):
    place_at = 0
    code_at = place_at + group * n_cols
    flag_at = code_at + group
    last = EXPERTS - 1

    def kernel(spot, hosts, out):
        me = spot[0]
        plane = lax.div(spot[1], group)
        lane = lax.rem(spot[1], group)
        for s in range(group):
            piece = lax.rem(lane + group - s, group)
            for k in range(n_cols):
                column = jnp.bitwise_xor(jnp.bitwise_and(me, n_cols - 1), k)
                out[place_at + s * n_cols + k] = piece * n_cols + column
        outer = jnp.where(plane < EXPERTS // 2, 0, last)
        inner = jnp.where(plane < EXPERTS // 2, 1, last - 1)
        near = jnp.int32(0)
        far = jnp.int32(0)
        for j in range(group):
            host = hosts[outer * group + j]
            near = jnp.where(host == inner, 1, near)
            far = jnp.where(host == last - outer, 1, far)
        at_end = jnp.where(plane == outer, 1, 0)
        for s in range(group):
            expert = hosts[plane * group + lax.rem(lane + s, group)]
            if two_slots:
                first = jnp.where(near == 1, inner, last - inner)
                code_end = jnp.where(expert == first, 2, 3)
                code_mid = jnp.where(expert == outer, 1, jnp.where(expert == last - plane, 4, 5))
                code = jnp.where(at_end == 1, code_end, code_mid)
            else:
                code = jnp.where(expert < plane, plane - expert, last + expert - plane)
            out[code_at + s] = jnp.where(expert == plane, 0, code)
        out[flag_at] = near
        out[flag_at + 1] = far
        out[flag_at + 2] = at_end
        out[flag_at + 3] = jnp.where(lane == lax.div(me, 2), 1, 0)

    table = pl.pallas_call(
        kernel,
        in_specs=[pl.BlockSpec(memory_space=pltpu.SMEM)] * 2,
        out_specs=pl.BlockSpec(memory_space=pltpu.SMEM),
        out_shape=jax.ShapeDtypeStruct((flag_at + 4,), jnp.int32),
        name="make_table",
    )(here, owner_expert)
    return table, place_at, code_at, flag_at


def body(
    grad_partials,
    master_weights,
    first_moment,
    second_moment,
    resident_weights,
    token_tiles,
    owner_expert,
    live_rows,
):
    n_dp = lax.axis_size("dp")
    n_expert = lax.axis_size("expert")
    group = n_expert // EXPERTS
    me = lax.axis_index("dp")
    own = lax.axis_index("expert")
    lane = own % group
    levels = n_dp.bit_length() - 1
    assert 1 << levels == n_dp and EXPERTS * group == n_expert

    rows, piece_cols = master_weights.shape
    owner_cols = resident_weights.shape[1]
    dp_cols = owner_cols // n_dp
    n_cols = piece_cols // dp_cols
    assert n_cols in (1, 2) and n_cols * dp_cols == piece_cols
    width = QB
    n_chunks = dp_cols // width
    parts = ROW_PARTS if rows % (ROW_PARTS * QB) == 0 else 1
    part_rows = rows // parts
    grad = grad_partials.reshape(n_dp * rows, piece_cols)
    state = (master_weights, first_moment, second_moment)

    two_slots = EXPERTS == 4 and group == 2
    here = jnp.stack([me, own]).astype(jnp.int32)
    table, place_at, code_at, flag_at = make_table(
        here, owner_expert, group, n_cols, two_slots
    )

    def flip(value, level):
        pairs = [(i, i ^ (1 << level)) for i in range(n_dp)]
        return lax.ppermute(value, "dp", pairs)

    def along(value, moves):
        pairs = [(a * group + j, b * group + j) for (a, b) in moves for j in range(group)]
        return lax.ppermute(value, "expert", pairs)

    columns = [[k * dp_cols + c * width for k in range(n_cols)] for c in range(n_chunks)]
    updated_master = None
    delta = [[None] * n_chunks for _ in range(parts)]

    def relative(level):
        return [(1 << level) + i * (2 << level) for i in range(n_dp >> (level + 1))]

    together = [[[h] for h in range(parts)] if c == 0 else [list(range(parts))] for c in range(n_chunks)]
    crossed_first = {}
    for c in range(n_chunks):
        for held in together[c]:
            held_rows = part_rows * len(held)
            first_part = held[0] // len(held)
            send = slab_sum(
                grad, here, relative(0), [], rows, held_rows, first_part, columns[c], width
            )
            crossed_first[c, held[0]] = flip(send, 0)
    for c in range(n_chunks):
        for held in together[c]:
            held_rows = part_rows * len(held)
            received = [(crossed_first[c, held[0]], 0)]
            for level in range(1, levels):
                feed = []
                for j, (array, offset) in enumerate(received):
                    feed.append(
                        (
                            array,
                            offset,
                            (1 << level) >> (j + 1),
                            (2 << level) >> (j + 1),
                        )
                    )
                send = slab_sum(
                    grad,
                    here,
                    relative(level),
                    feed,
                    rows,
                    held_rows,
                    held[0] // len(held),
                    columns[c],
                    width,
                )
                received.append((flip(send, level), 0))
            for h in held:
                updated_master, changes = adam_parts(
                    grad,
                    here,
[(array, h - held[0]) for array, _ in received],
                    state,
                    updated_master,
                    rows,
                    part_rows,
                    [h],
                    columns[c],
                    width,
                )
                delta[h][c] = changes[0]

    last = EXPERTS - 1

    def at(index):
        return lambda tab: tab[index]

    def full_line(pieces):
        found = []
        for piece in pieces:
            options = [piece]
            for side in range(2):
                value = piece
                for k in range(1, EXPERTS):
                    moves = [(p, p + 1) for p in range(k - 1, last)]
                    if side:
                        moves = [(last - a, last - b) for a, b in moves]
                    value = along(value, moves)
                    options.append(value)
            found.append(options)
        return found

    def slotted_line(pieces):
        sides = [(0, 1), (1, 0), (2, 3), (3, 2)]
        middle = [(1, 2), (2, 1)]
        count = len(pieces)
        side, center = [], []

        def odd_code(tab):
            return 1 - tab[flag_at]

        def even_code(tab):
            return jnp.where(tab[flag_at + 2] == 1, 2, tab[flag_at + 1])

        def last_code(tab):
            return tab[flag_at + 1]

        for t in range(2 * count + 1):
            c = t // 2
            if t == 0:
                value = pieces[0]
            else:
                if t % 2:
                    value = pick(table, odd_code, [[pieces[c], center[2 * c]]])
                elif c < count:
                    choices = [center[t - 2], center[t - 1], pieces[c]]
                    value = pick(table, even_code, [choices])
                else:
                    value = pick(table, last_code, [[center[t - 2], center[t - 1]]])
            side.append(along(value, sides))
            if t < 2 * count:
                center.append(along(side[t - 1] if t % 2 else pieces[c], middle))
        return [
            [pieces[c], *side[2 * c : 2 * c + 3], *center[2 * c : 2 * c + 2]] for c in range(count)
        ]

    if two_slots:
        options = [slotted_line(delta[h]) for h in range(parts)]
    else:
        options = [full_line(delta[h]) for h in range(parts)]

    moved = [[[None] * parts for _ in range(n_chunks)] for _ in range(group)]
    for c in range(n_chunks):
        groups = [[h] for h in range(parts)] if c == n_chunks - 1 else [list(range(parts))]
        for held in groups:
            for s in range(1, group):
                value = pick(table, at(code_at + s), [options[h][c] for h in held])
                pairs = [
                    (e * group + j, e * group + (j + s) % group)
                    for e in range(EXPERTS)
                    for j in range(group)
                ]
                value = lax.ppermute(value, "expert", pairs)
                for h in held:
                    moved[s][c][h] = (value, (h - held[0]) * part_rows)

    def piece_of(c, s):
        if s == 0:
            sources = [[(array, 0) for array in options[h][c]] for h in range(parts)]
            code_of = at(code_at)
        else:
            sources, code_of = [[moved[s][c][h]] for h in range(parts)], lambda tab: 0
        return sources, code_of, [place_at + s * n_cols + k for k in range(n_cols)]

    sums = []
    parity = (me % 2).astype(jnp.int32)
    for c in range(n_chunks):
        pieces = [piece_of(c, s) for s in range(group)]
        groups = [[piece] for piece in pieces]
        results = []
        for chosen in groups:
            results.append(
                serve(token_tiles, resident_weights, chosen, table, part_rows, n_chunks, c, width)
            )
        if n_dp == 4 and group == 2:
            kept = []
            for straight_sums, crossed_sums in results:
                crossed = flip(crossed_sums, 0)
                for s in range(straight_sums.shape[0]):
                    kept.append(straight_sums[s].astype(jnp.float32) + crossed[s].astype(jnp.float32))
            straight = table[flag_at + 3] == 1
            other = jnp.where(straight, kept[1], kept[0]).astype(jnp.bfloat16)
            held = jnp.where(straight, kept[0], kept[1])
            crossed = flip(other, 1)
            sums.append(held + crossed.astype(jnp.float32))
        else:
            products = [
                [result[k][s] for k in range(n_cols)]
                for result in results
                for s in range(result[0].shape[0])
            ]
            buffer = jnp.zeros((n_dp,) + products[0][0].shape, jnp.bfloat16)
            for s in range(group):
                piece = (lane - s) % group
                for k in range(n_cols):
                    column = piece * n_cols + ((k ^ parity) if n_cols == 2 else 0)
                    buffer = lax.dynamic_update_index_in_dim(
                        buffer, products[s][k], jnp.bitwise_xor(column, me), 0
                    )
            for level in range(levels):
                got = flip(buffer[1::2], level).astype(jnp.float32)
                buffer = (buffer[0::2].astype(jnp.float32) + got).astype(
                    jnp.bfloat16 if level < levels - 1 else jnp.float32
                )
            sums.append(buffer[0])
    summed = jnp.concatenate(sums, axis=1)
    row_index = lax.broadcasted_iota(jnp.int32, summed.shape, 0)
    projected = jnp.where(row_index < live_rows[0], summed, jnp.float32(0.0)).astype(jnp.bfloat16)
    return (updated_master, projected)


def solution(mesh):
    placed = (
        P("dp", None, "expert"),
        P("dp", "expert"),
        P("dp", "expert"),
        P("dp", "expert"),
        P("dp", "expert"),
        P("expert", "dp"),
        P(),
        P("expert"),
    )

    return jax.shard_map(
        body,
        mesh=mesh,
        in_specs=placed,
        out_specs=(P("dp", "expert"), P("expert", "dp")),
        check_vma=False,
    )
```

```python
import jax
import jax.numpy as jnp
from jax import lax
from jax.experimental import pallas as pl
from jax.experimental.pallas import tpu as pltpu
from jax.sharding import PartitionSpec as P


EXPERTS = 4
QB = 128

beta_first = 0.9
beta_second = 0.95
learn_rate = 0.02
decay_rate = 0.1
adam_epsilon = 1e-08
scale_epsilon = 1e-06
quant_range = 448.0
grid_step = 8.0
bias_first = 1.0 - 0.9**20
bias_second = 1.0 - 0.95**20

ROW_PARTS = 2
TILE = 1024
UNROLL = 7
SUM_VMEM = 50 << 20
PICK_VMEM = 16 << 20
ADAM_VMEM = 57 << 20
SERVE_VMEM = 50 << 20


def adamw(gradient, master_weights, first_moment, second_moment):
    moment_one = beta_first * first_moment + (1.0 - beta_first) * gradient
    moment_two = beta_second * second_moment + (1.0 - beta_second) * gradient * gradient
    update = (moment_one * (1.0 / bias_first)) / (
        jnp.sqrt(moment_two * (1.0 / bias_second)) + adam_epsilon
    )
    return master_weights - learn_rate * (update + decay_rate * master_weights)


def params(limit):
    return pltpu.CompilerParams(vmem_limit_bytes=limit)


def total(refs):
    value = refs[0].astype(jnp.float32)
    for ref in refs[1:]:
        value = value + ref.astype(jnp.float32)
    return value


def slab_sum(grad, table, relative, received, rows, part_rows, part, cols, width):
    n_out = len(relative)
    skip = relative[1] - relative[0] if n_out > 1 else 0
    n_cols = len(cols)
    block = part_rows
    step = rows // block
    n_rows = part_rows // block

    def kernel(tab, *refs):
        grads, recs, out = refs[:n_cols], refs[n_cols:-1], refs[-1]
        for k in range(n_cols):
            span = slice(k * width, (k + 1) * width)
            values = [grads[k][...]] + [rec[0, :, span] for rec in recs]
            out[0, :, span] = total(values).astype(out.dtype)

    def grad_map(k):
        at = cols[k] // width
        return lambda i, r, tab: (jnp.bitwise_xor(tab[0], relative[0] + i * skip) * step + part * n_rows + r, at)

    def rec_map(stride, offset, first):
        return lambda i, r, tab: (first + i * stride, offset * n_rows + r, 0)

    in_specs = [pl.BlockSpec((block, width), grad_map(k)) for k in range(n_cols)]
    in_specs += [
        pl.BlockSpec((1, block, n_cols * width), rec_map(stride, offset, first))
        for (_, offset, first, stride) in received
    ]
    moved = n_out * part_rows * n_cols * width * 2
    return pl.pallas_call(
        kernel,
        grid_spec=pltpu.PrefetchScalarGridSpec(
            num_scalar_prefetch=1,
            grid=(n_out, n_rows),
            in_specs=in_specs,
            out_specs=pl.BlockSpec((1, block, n_cols * width), lambda i, r, tab: (i, r, 0)),
        ),
        out_shape=jax.ShapeDtypeStruct((n_out, part_rows, n_cols * width), jnp.bfloat16),
        compiler_params=params(SUM_VMEM),
        cost_estimate=pl.CostEstimate(
            flops=moved, bytes_accessed=moved * (2 + len(received)), transcendentals=0
        ),
        name="slab_sum",
    )(table, *([grad] * n_cols), *[item[0] for item in received])


def adam_parts(grad, table, received, state, out, rows, part_rows, parts, cols, width):
    n_cols = len(cols)
    block = part_rows
    step = rows // block
    n_parts = len(parts)
    first_part = parts[0]
    base = cols[0] // width
    stride = (cols[1] - cols[0]) // width if n_cols > 1 else 0
    n_rec = len(received)

    def kernel(tab, grad_ref, *refs):
        recs = refs[:n_rec]
        master, first, second = refs[n_rec : n_rec + 3]
        new_ref = refs[-1 - n_parts]
        deltas = refs[-n_parts:]
        gradient = total([grad_ref[...]] + [rec[0] for rec in recs])
        old = master[...]
        new = adamw(gradient, old, first[...], second[...])
        new_ref[...] = new
        change = (new - old).astype(jnp.bfloat16)
        if n_parts == 1:
            deltas[0][...] = change
        else:
            for h in range(n_parts):

                @pl.when(pl.program_id(0) == h)
                def _():
                    deltas[h][...] = change

    def state_map(r, k, tab):
        return (first_part + r, base + k * stride)

    state_spec = pl.BlockSpec((block, width), state_map)
    in_specs = [
        pl.BlockSpec((block, width), lambda r, k, tab: (tab[0] * step + first_part + r, base + k * stride))
    ]

    def rec_map(offset):
        return lambda r, k, tab: (0, offset + r, k)

    def delta_map(h):
        return lambda r, k, tab: (0, jnp.where(r == h, k, jnp.where(r < h, 0, n_cols - 1)))

    in_specs += [pl.BlockSpec((1, block, width), rec_map(offset)) for (_, offset) in received]
    in_specs += [state_spec] * 3
    operands = [table, grad, *[item[0] for item in received], *state]
    aliases = {}
    if out is not None:
        in_specs.append(pl.BlockSpec(memory_space=pl.ANY))
        aliases = {len(operands): 0}
        operands.append(out)
    count = n_parts * part_rows * n_cols * width
    result = pl.pallas_call(
        kernel,
        grid_spec=pltpu.PrefetchScalarGridSpec(
            num_scalar_prefetch=1,
            grid=(n_parts, n_cols),
            in_specs=in_specs,
            out_specs=(
                state_spec,
                *[pl.BlockSpec((block, width), delta_map(h)) for h in range(n_parts)],
            ),
        ),
        out_shape=(
            jax.ShapeDtypeStruct(state[0].shape, jnp.float32),
            *[jax.ShapeDtypeStruct((part_rows, n_cols * width), jnp.bfloat16)] * n_parts,
        ),
        input_output_aliases=aliases,
        compiler_params=params(ADAM_VMEM),
        cost_estimate=pl.CostEstimate(
            flops=30 * count, bytes_accessed=(20 + 2 * n_rec) * count, transcendentals=2 * count
        ),
        name="adam_parts",
    )(*operands)
    return result[0], result[1:]


def pick(table, code_of, parts):
    cols = parts[0][1][0][0].shape[1]
    n_options = len(parts[0][1])
    starts = [sum(rows for rows, _ in parts[:p]) for p in range(len(parts) + 1)]
    shape = (starts[-1], cols)

    def kernel(tab, *refs):
        out, sems = refs[-2:]
        code = code_of(tab)
        for k in range(n_options):

            @pl.when(code == k)
            def _():
                copies = [
                    pltpu.make_async_copy(
                        refs[p * n_options + k].at[pl.ds(options[k][1], rows)],
                        out.at[pl.ds(starts[p], rows)],
                        sems.at[p],
                    )
                    for p, (rows, options) in enumerate(parts)
                ]
                for copy in copies:
                    copy.start()
                for copy in copies:
                    copy.wait()

    operands = [array for _, options in parts for array, _ in options]
    return pl.pallas_call(
        kernel,
        grid_spec=pltpu.PrefetchScalarGridSpec(
            num_scalar_prefetch=1,
            grid=(1,),
            in_specs=[pl.BlockSpec(memory_space=pl.ANY)] * len(operands),
            out_specs=pl.BlockSpec(shape, lambda i, tab: (0, 0)),
            scratch_shapes=[pltpu.SemaphoreType.DMA((len(parts),))],
        ),
        out_shape=jax.ShapeDtypeStruct(shape, jnp.bfloat16),
        compiler_params=params(PICK_VMEM),
        cost_estimate=pl.CostEstimate(
            flops=0, bytes_accessed=4 * shape[0] * shape[1], transcendentals=0
        ),
        name="pick",
    )(table, *operands)


def serve(tokens, resident, pieces, table, stride, shift, width):
    rows_total, depth = tokens.shape
    n_pieces = len(pieces)
    n_parts = max(len(parts) for parts, _, _ in pieces)
    part_cols = pieces[0][0][0][2][0][0].shape[1]
    n_cols = part_cols // width
    tile = TILE if rows_total % TILE == 0 else rows_total

    def kernel(tab, tokens_ref, resident_ref, *refs):
        outs = refs[-7 - n_cols : -7]
        tok, held, weight, delta, sems, held_sems, tok_sem = refs[-7:]
        at_ref = 0

        def fetch_resident(s, k):
            column = (tab[pieces[s][2][k]] * stride + shift) * width
            return pltpu.make_async_copy(
                resident_ref.at[:, pl.ds(pl.multiple_of(column, width), width)],
                held.at[s, k],
                held_sems.at[s, k],
            )

        fetch_tokens = pltpu.make_async_copy(tokens_ref, tok, tok_sem)

        def fetch(s, p, ref=None):
            first, rows, _ = pieces[s][0][p]
            target = delta.at[s, pl.ds(first, rows)]
            return pltpu.make_async_copy(target if ref is None else ref, target, sems.at[s, p])

        for s, (parts, code_of, _) in enumerate(pieces):
            code = code_of(tab)
            n_options = len(parts[0][2])
            for k in range(n_options):
                chosen = [
                    refs[at_ref + p * n_options + k].at[pl.ds(options[k][1], rows)]
                    for p, (_, rows, options) in enumerate(parts)
                ]

                @pl.when(code == k)
                def _():
                    for p, ref in enumerate(chosen):
                        fetch(s, p, ref).start()

            at_ref += len(parts) * n_options
            for k in range(n_cols):
                fetch_resident(s, k).start()
        fetch_tokens.start()
        for s, (parts, _, places) in enumerate(pieces):
            starts = [
                pl.multiple_of(lax.rem(tab[places[k]], n_cols) * width, width)
                for k in range(n_cols)
            ]
            for k in range(n_cols):
                fetch_resident(s, k).wait()
            for p in range(len(parts)):
                fetch(s, p).wait()

            @pl.loop(0, depth // QB, unroll=UNROLL)
            def _(b):
                at = pl.multiple_of(b * QB, QB)
                for k in range(n_cols):
                    for c in range(width // QB):
                        span = slice(c * QB, (c + 1) * QB)
                        change = delta[s, pl.ds(at, QB), pl.ds(starts[k] + c * QB, QB)]
                        value = held[s, k, pl.ds(at, QB), span].astype(
                            jnp.float32
                        ) + change.astype(jnp.float32)
                        largest = jnp.max(jnp.abs(value), axis=(0, 1), keepdims=True)
                        scale = (largest + scale_epsilon) / quant_range
                        level = jnp.floor(value * (1.0 / (scale * grid_step)) + 0.5)
                        column = (s * n_cols + k) * width + c * QB
                        weight[pl.ds(at, QB), column : column + QB] = (
                            level * (scale * grid_step)
                        ).astype(jnp.bfloat16)

        fetch_tokens.wait()

        @pl.loop(0, rows_total // tile)
        def _(m):
            at = pl.multiple_of(m * tile, tile)
            product = jnp.dot(
                tok[pl.ds(at, tile), :], weight[...], preferred_element_type=jnp.float32
            )
            for s in range(n_pieces):
                for k in range(n_cols):
                    column = (s * n_cols + k) * width
                    outs[k][s, pl.ds(at, tile), :] = product[:, column : column + width].astype(
                        jnp.bfloat16
                    )

    in_specs = [pl.BlockSpec(memory_space=pl.ANY)] * 2
    operands = [tokens, resident]
    for parts, _, _ in pieces:
        for _, _, options in parts:
            in_specs += [pl.BlockSpec(memory_space=pl.ANY)] * len(options)
            operands += [array for array, _ in options]
    out_spec = pl.BlockSpec((n_pieces, rows_total, width), lambda i, tab: (0, 0, 0))
    out_shape = jax.ShapeDtypeStruct((n_pieces, rows_total, width), jnp.bfloat16)
    return pl.pallas_call(
        kernel,
        grid_spec=pltpu.PrefetchScalarGridSpec(
            num_scalar_prefetch=1,
            grid=(1,),
            in_specs=in_specs,
            out_specs=(out_spec,) * n_cols,
            scratch_shapes=[
                pltpu.VMEM((rows_total, depth), jnp.bfloat16),
                pltpu.VMEM((n_pieces, n_cols, depth, width), jnp.bfloat16),
                pltpu.VMEM((depth, n_pieces * n_cols * width), jnp.bfloat16),
                pltpu.VMEM((n_pieces, depth, part_cols), jnp.bfloat16),
                pltpu.SemaphoreType.DMA((n_pieces, n_parts)),
                pltpu.SemaphoreType.DMA((n_pieces, n_cols)),
                pltpu.SemaphoreType.DMA,
            ],
        ),
        out_shape=(out_shape,) * n_cols,
        compiler_params=params(SERVE_VMEM),
        cost_estimate=pl.CostEstimate(
            flops=2 * rows_total * depth * n_pieces * n_cols * width,
            bytes_accessed=2 * depth * (rows_total + 2 * n_pieces * n_cols * width),
            transcendentals=0,
        ),
        name="serve",
    )(table, *operands)


def make_table(here, owner_expert, group, n_cols, two_slots):
    place_at = 0
    code_at = place_at + group * n_cols
    flag_at = code_at + group
    last = EXPERTS - 1

    def kernel(spot, hosts, out):
        me = spot[0]
        plane = lax.div(spot[1], group)
        lane = lax.rem(spot[1], group)
        for s in range(group):
            piece = lax.rem(lane + group - s, group)
            for k in range(n_cols):
                column = jnp.bitwise_xor(jnp.bitwise_and(me, n_cols - 1), k)
                out[place_at + s * n_cols + k] = piece * n_cols + column
        outer = jnp.where(plane < EXPERTS // 2, 0, last)
        inner = jnp.where(plane < EXPERTS // 2, 1, last - 1)
        near = jnp.int32(0)
        far = jnp.int32(0)
        for j in range(group):
            host = hosts[outer * group + j]
            near = jnp.where(host == inner, 1, near)
            far = jnp.where(host == last - outer, 1, far)
        at_end = jnp.where(plane == outer, 1, 0)
        for s in range(group):
            expert = hosts[plane * group + lax.rem(lane + s, group)]
            if two_slots:
                first = jnp.where(near == 1, inner, last - inner)
                code_end = jnp.where(expert == first, 2, 3)
                code_mid = jnp.where(expert == outer, 1, jnp.where(expert == last - plane, 4, 5))
                code = jnp.where(at_end == 1, code_end, code_mid)
            else:
                code = jnp.where(expert < plane, plane - expert, last + expert - plane)
            out[code_at + s] = jnp.where(expert == plane, 0, code)
        out[flag_at] = near
        out[flag_at + 1] = far
        out[flag_at + 2] = at_end
        out[flag_at + 3] = jnp.where(lane == lax.div(me, 2), 1, 0)

    table = pl.pallas_call(
        kernel,
        in_specs=[pl.BlockSpec(memory_space=pltpu.SMEM)] * 2,
        out_specs=pl.BlockSpec(memory_space=pltpu.SMEM),
        out_shape=jax.ShapeDtypeStruct((flag_at + 4,), jnp.int32),
        name="make_table",
    )(here, owner_expert)
    return table, place_at, code_at, flag_at


def body(
    grad_partials,
    master_weights,
    first_moment,
    second_moment,
    resident_weights,
    token_tiles,
    owner_expert,
    live_rows,
):
    n_dp = lax.axis_size("dp")
    n_expert = lax.axis_size("expert")
    group = n_expert // EXPERTS
    me = lax.axis_index("dp")
    own = lax.axis_index("expert")
    lane = own % group
    levels = n_dp.bit_length() - 1
    assert 1 << levels == n_dp and EXPERTS * group == n_expert

    rows, piece_cols = master_weights.shape
    owner_cols = resident_weights.shape[1]
    dp_cols = owner_cols // n_dp
    n_cols = piece_cols // dp_cols
    assert n_cols in (1, 2) and n_cols * dp_cols == piece_cols
    width = QB
    n_chunks = dp_cols // width
    parts = ROW_PARTS if rows % (ROW_PARTS * QB) == 0 else 1
    part_rows = rows // parts
    grad = grad_partials.reshape(n_dp * rows, piece_cols)
    state = (master_weights, first_moment, second_moment)

    two_slots = EXPERTS == 4 and group == 2
    here = jnp.stack([me, own]).astype(jnp.int32)
    table, place_at, code_at, flag_at = make_table(
        here, owner_expert, group, n_cols, two_slots
    )

    def flip(value, level):
        pairs = [(i, i ^ (1 << level)) for i in range(n_dp)]
        return lax.ppermute(value, "dp", pairs)

    def along(value, moves):
        pairs = [(a * group + j, b * group + j) for (a, b) in moves for j in range(group)]
        return lax.ppermute(value, "expert", pairs)

    columns = [[k * dp_cols + c * width for k in range(n_cols)] for c in range(n_chunks)]
    updated_master = None
    delta = [[None] * n_chunks for _ in range(parts)]

    def relative(level):
        return [(1 << level) + i * (2 << level) for i in range(n_dp >> (level + 1))]

    together = [[[h] for h in range(parts)] if c == 0 else [list(range(parts))] for c in range(n_chunks)]
    crossed_first = {}
    for c in range(n_chunks):
        for held in together[c]:
            held_rows = part_rows * len(held)
            first_part = held[0] // len(held)
            send = slab_sum(
                grad, here, relative(0), [], rows, held_rows, first_part, columns[c], width
            )
            crossed_first[c, held[0]] = flip(send, 0)
    for c in range(n_chunks):
        for held in together[c]:
            held_rows = part_rows * len(held)
            received = [(crossed_first[c, held[0]], 0)]
            for level in range(1, levels):
                feed = []
                for j, (array, offset) in enumerate(received):
                    feed.append(
                        (
                            array,
                            offset,
                            (1 << level) >> (j + 1),
                            (2 << level) >> (j + 1),
                        )
                    )
                send = slab_sum(
                    grad,
                    here,
                    relative(level),
                    feed,
                    rows,
                    held_rows,
                    held[0] // len(held),
                    columns[c],
                    width,
                )
                received.append((flip(send, level), 0))
            for h in held:
                updated_master, changes = adam_parts(
                    grad,
                    here,
[(array, h - held[0]) for array, _ in received],
                    state,
                    updated_master,
                    rows,
                    part_rows,
                    [h],
                    columns[c],
                    width,
                )
                delta[h][c] = changes[0]

    def entire(arrays, first=0):
        return [(array, first) for array in arrays]

    last = EXPERTS - 1

    def at(index):
        return lambda tab: tab[index]

    def full_line(pieces):
        found = []
        for piece in pieces:
            options = [piece]
            for side in range(2):
                value = piece
                for k in range(1, EXPERTS):
                    moves = [(p, p + 1) for p in range(k - 1, last)]
                    if side:
                        moves = [(last - a, last - b) for a, b in moves]
                    value = along(value, moves)
                    options.append(value)
            found.append([(part_rows, entire(options))])
        return found

    def slotted_line(pieces, h):
        sides = [(0, 1), (1, 0), (2, 3), (3, 2)]
        middle = [(1, 2), (2, 1)]
        count = len(pieces)
        side, center = [], []

        def odd_code(tab):
            return 1 - tab[flag_at]

        def even_code(tab):
            return jnp.where(tab[flag_at + 2] == 1, 2, tab[flag_at + 1])

        def last_code(tab):
            return tab[flag_at + 1]

        near_rows = (part_rows // QB + 1) // 2 * QB if h == parts - 1 else part_rows
        cuts = [(0, near_rows), (near_rows, part_rows - near_rows)]
        cuts = [cut for cut in cuts if cut[1]]
        for t in range(2 * count):
            c = t // 2
            if t == 0:
                value = pieces[0]
            else:
                if t % 2:
                    choices = [pieces[c], center[2 * c]]
                    value = pick(table, odd_code, [(part_rows, entire(choices))])
                else:
                    choices = [center[t - 2], center[t - 1], pieces[c]]
                    value = pick(table, even_code, [(part_rows, entire(choices))])
            side.append(along(value, sides))
            center.append(along(side[t - 1] if t % 2 else pieces[c], middle))
        ends = []
        for first, n_rows in cuts:
            value = pick(table, last_code, [(n_rows, entire(center[-2:], first))])
            ends.append(along(value, sides))
        found = []
        for c in range(count):
            rest = center[2 * c : 2 * c + 2]
            if c < count - 1:
                arrays = [pieces[c], *side[2 * c : 2 * c + 3], *rest]
                found.append([(part_rows, entire(arrays))])
            else:
                found.append(
                    [
                        (
                            n_rows,
                            entire([pieces[c], *side[2 * c : 2 * c + 2]], first)
                            + [(end, 0)]
                            + entire(rest, first),
                        )
                        for (first, n_rows), end in zip(cuts, ends)
                    ]
                )
        return found

    if two_slots:
        options = [slotted_line(delta[h], h) for h in range(parts)]
    else:
        options = [full_line(delta[h]) for h in range(parts)]

    chunk_parts = [[part for h in range(parts) for part in options[h][c]] for c in range(n_chunks)]
    moved = [[[] for _ in range(n_chunks)] for _ in range(group)]
    for c in range(n_chunks):
        split = c == n_chunks - 1
        groups = [[part] for part in chunk_parts[c]] if split else [chunk_parts[c]]
        for held in groups:
            for s in range(1, group):
                value = pick(table, at(code_at + s), held)
                pairs = [
                    (e * group + j, e * group + (j + s) % group)
                    for e in range(EXPERTS)
                    for j in range(group)
                ]
                value = lax.ppermute(value, "expert", pairs)
                moved[s][c].append((value.shape[0], [(value, 0)]))

    def placed(parts_of):
        first, found = 0, []
        for n_rows, choices in parts_of:
            found.append((first, n_rows, choices))
            first += n_rows
        return found

    def piece_of(c, s):
        places = [place_at + s * n_cols + k for k in range(n_cols)]
        if s == 0:
            return placed(chunk_parts[c]), at(code_at), places
        return placed(moved[s][c]), lambda tab: 0, places

    sums = []
    parity = (me % 2).astype(jnp.int32)
    for c in range(n_chunks):
        pieces = [piece_of(c, s) for s in range(group)]
        groups = [pieces] if c == n_chunks - 1 else [[piece] for piece in pieces]
        results = []
        for chosen in groups:
            results.append(serve(token_tiles, resident_weights, chosen, table, n_chunks, c, width))
        if n_dp == 4 and group == 2:
            kept = []
            for straight_sums, crossed_sums in results:
                crossed = flip(crossed_sums, 0)
                for s in range(straight_sums.shape[0]):
                    kept.append(straight_sums[s].astype(jnp.float32) + crossed[s].astype(jnp.float32))
            straight = table[flag_at + 3] == 1
            other = jnp.where(straight, kept[1], kept[0]).astype(jnp.bfloat16)
            held = jnp.where(straight, kept[0], kept[1])
            crossed = flip(other, 1)
            sums.append(held + crossed.astype(jnp.float32))
        else:
            products = [
                [result[k][s] for k in range(n_cols)]
                for result in results
                for s in range(result[0].shape[0])
            ]
            buffer = jnp.zeros((n_dp,) + products[0][0].shape, jnp.bfloat16)
            for s in range(group):
                piece = (lane - s) % group
                for k in range(n_cols):
                    column = piece * n_cols + ((k ^ parity) if n_cols == 2 else 0)
                    buffer = lax.dynamic_update_index_in_dim(
                        buffer, products[s][k], jnp.bitwise_xor(column, me), 0
                    )
            for level in range(levels):
                got = flip(buffer[1::2], level).astype(jnp.float32)
                buffer = (buffer[0::2].astype(jnp.float32) + got).astype(
                    jnp.bfloat16 if level < levels - 1 else jnp.float32
                )
            sums.append(buffer[0])
    summed = jnp.concatenate(sums, axis=1)
    row_index = lax.broadcasted_iota(jnp.int32, summed.shape, 0)
    projected = jnp.where(row_index < live_rows[0], summed, jnp.float32(0.0)).astype(jnp.bfloat16)
    return (updated_master, projected)


def solution(mesh):
    placed = (
        P("dp", None, "expert"),
        P("dp", "expert"),
        P("dp", "expert"),
        P("dp", "expert"),
        P("dp", "expert"),
        P("expert", "dp"),
        P(),
        P("expert"),
    )

    return jax.shard_map(
        body,
        mesh=mesh,
        in_specs=placed,
        out_specs=(P("dp", "expert"), P("expert", "dp")),
        check_vma=False,
    )
```
